32 devices in a mesh: dp: 4 (over y, core), mp: 8 (over z, x).
Axes of the slice: x: 2, y: 2, z: 4, core: 2. Of those that a mesh axis runs over, the one named last changes fastest.
Arguments:
- tokens: bfloat16 [768, 8192], P('dp', 'mp'), may hold values from -6 to 6
- out_grad: bfloat16 [768, 8192], P('dp', 'mp'), may hold values from -6 to 6
- w_gate: bfloat16 [8, 96, 128, 128], P('mp'), may hold values from -0.125 to 0.125
- w_up: bfloat16 [8, 96, 128, 128], P('mp'), may hold values from -0.125 to 0.125
- w_down: bfloat16 [8, 96, 128, 128], P('mp'), may hold values from -0.125 to 0.125
- gu_rows: int32 [8, 96], P('mp'), may hold values from 0 to 63, as said below
- gu_cols: int32 [8, 96], P('mp'), may hold values from 0 to 6
- gu_count: int32 [8], P('mp'), may hold values from 24 to 96, as said below
- dn_rows: int32 [8, 96], P('mp'), may hold values from 0 to 6, as said below
- dn_cols: int32 [8, 96], P('mp'), may hold values from 0 to 63
- dn_count: int32 [8], P('mp'), may hold values from 24 to 96, as said below
Outputs:
- ffn_out: bfloat16 [768, 8192], P('dp', 'mp')
- input_grad: bfloat16 [768, 8192], P('dp', 'mp')
- gate_step: float32 [8, 96, 128, 128], P('mp', 'dp')
- up_step: float32 [8, 96, 128, 128], P('mp', 'dp')
- down_step: float32 [8, 96, 128, 128], P('mp', 'dp')
The draws below stay inside these ranges and needn't reach their ends.
Inputs may be any that keep to these rules, and one draw needn't show every extreme that they name: Pairs (gu_rows, gu_cols) are distinct within one mp index, slots that are not live included. `gu_count`: some mp index has all 96 slots live. Pairs (dn_rows, dn_cols) are distinct within one mp index, slots that are not live included. `dn_count`: some mp index has all 96 slots live.
All inputs are finite; a program needn't handle non-finite values.
Results may differ from the reference program's by a relative error of at most 0.012.
Values may be sent and summed in bfloat16 or wider, within the bound.
A program may use at most 128 MiB of HBM per device.

```python
import math
import jax
import jax.numpy as jnp
from jax import lax

D = 8192
BLK = 128
HID_DEV = 896
MAXB = 96
TOK_DEV = 192
FF = 7168
TOKENS = 768
N_DP = 4
N_MP = 8


def live_blocks(key, salt):
    key = jax.random.fold_in(key, salt)
    key_perm, key_count, key_top = jax.random.split(key, 3)
    candidates = D // BLK * (HID_DEV // BLK)
    picks = jax.vmap(lambda k: jax.random.permutation(k, candidates))(jax.random.split(key_perm, N_MP))
    picks = picks[:, :MAXB]
    counts = jax.random.randint(key_count, (N_MP,), MAXB // 4, MAXB + 1)
    top_index = jax.random.randint(key_top, (), 0, N_MP)
    counts = jnp.where(jnp.arange(N_MP) == top_index, MAXB, counts)
    return (picks.astype(jnp.int32), counts.astype(jnp.int32))


def draw_gu_rows(key, part):
    picks, counts = live_blocks(key, 11)
    return picks // (HID_DEV // BLK)


def draw_gu_cols(key, part):
    picks, counts = live_blocks(key, 11)
    return picks % (HID_DEV // BLK)


def draw_gu_count(key, part):
    picks, counts = live_blocks(key, 11)
    return counts


def draw_dn_rows(key, part):
    picks, counts = live_blocks(key, 23)
    return picks % (HID_DEV // BLK)


def draw_dn_cols(key, part):
    picks, counts = live_blocks(key, 23)
    return picks // (HID_DEV // BLK)


def draw_dn_count(key, part):
    picks, counts = live_blocks(key, 23)
    return counts


def level_of(key, shape, cuts, least, top_value):
    gain, own = 1.0, jax.random.fold_in(key, 6)
    for axis_at, blocks in cuts:
        steps = jnp.exp(jax.random.uniform(jax.random.fold_in(own, axis_at), (blocks,), jnp.float32, least / len(cuts), top_value / len(cuts)))
        gain = gain * jnp.repeat(steps, shape[axis_at] // blocks).reshape([-1 if axis == axis_at else 1 for axis in range(len(shape))])
    return gain


def normal_values(stream_key, shape, deviation, most, shards=(), kind=jnp.bfloat16):
    drawn = deviation * jax.random.normal(stream_key, shape, jnp.float32)
    if shards:
        drawn = drawn * level_of(stream_key, shape, shards, -0.22, 0.18)
    return jnp.clip(drawn, -most, most).astype(kind)


def setup_inputs(seed: int = 0) -> dict:
    key_of = jax.random.split(jax.random.key(seed), 12)
    return {
        "tokens": normal_values(key_of[0], (TOKENS, D), 1.0, 6.0, ((0, 4), (1, 8))),
        "out_grad": normal_values(key_of[1], (TOKENS, D), 1.0, 6.0, ((0, 4), (1, 8))),
        "w_gate": normal_values(key_of[2], (N_MP, MAXB, BLK, BLK), (D // 4) ** -0.5, 0.125, ((0, 8),)),
        "w_up": normal_values(key_of[3], (N_MP, MAXB, BLK, BLK), (D // 4) ** -0.5, 0.125, ((0, 8),)),
        "w_down": normal_values(key_of[4], (N_MP, MAXB, BLK, BLK), (FF // 4) ** -0.5, 0.125, ((0, 8),)),
        "gu_rows": draw_gu_rows(jax.random.fold_in(key_of[11], 71), 0),
        "gu_cols": draw_gu_cols(jax.random.fold_in(key_of[11], 71), 0),
        "gu_count": draw_gu_count(jax.random.fold_in(key_of[11], 71), 0),
        "dn_rows": draw_dn_rows(jax.random.fold_in(key_of[11], 71), 0),
        "dn_cols": draw_dn_cols(jax.random.fold_in(key_of[11], 71), 0),
        "dn_count": draw_dn_count(jax.random.fold_in(key_of[11], 71), 0),
    }


decay_coef = 8.0

def place(count_rows, blocks, index, tiles):
    return jnp.zeros((tiles.shape[0], count_rows, blocks), jnp.float32).at[:, index, :].add(tiles)

def reference(tokens, out_grad, w_gate, w_up, w_down, gu_rows, gu_cols, gu_count, dn_rows, dn_cols, dn_count):
    hi = lax.Precision.HIGHEST
    dblocks = D // BLK
    hblocks = HID_DEV // BLK
    ntok = tokens.shape[0]
    x_blocks = tokens.astype(jnp.float32).reshape(ntok, dblocks, BLK)
    dy_blocks = out_grad.astype(jnp.float32).reshape(ntok, dblocks, BLK)
    scale_root = 1.0 / math.sqrt(TOKENS)
    slot_ids = jnp.arange(MAXB)

    def group_grad(left, right):
        left_g = left.reshape(N_DP, TOK_DEV, MAXB, BLK)
        right_g = right.reshape(N_DP, TOK_DEV, MAXB, BLK)
        parts = jnp.einsum('dtsk,dtsn->dskn', left_g, right_g, precision=hi).astype(jnp.bfloat16)
        parts = lax.optimization_barrier(parts)
        return lax.optimization_barrier(jnp.sum(parts.astype(jnp.float32), axis=0))

    def one_device(carry, m):
        out_total, in_total = carry
        wg = w_gate[m].astype(jnp.float32)
        wu = w_up[m].astype(jnp.float32)
        wd = w_down[m].astype(jnp.float32)
        rows = gu_rows[m]
        cols = gu_cols[m]
        drows = dn_rows[m]
        dcols = dn_cols[m]
        live = (slot_ids < gu_count[m]).astype(jnp.float32)
        dlive = (slot_ids < dn_count[m]).astype(jnp.float32)
        xt = x_blocks[:, rows, :]
        gate = place(hblocks, BLK, cols, jnp.einsum('tsk,skn->tsn', xt, wg, precision=hi) * live[None, :, None])
        up = place(hblocks, BLK, cols, jnp.einsum('tsk,skn->tsn', xt, wu, precision=hi) * live[None, :, None])
        sig = jax.nn.sigmoid(gate)
        act = gate * sig
        hidden = (act * up).astype(jnp.bfloat16).astype(jnp.float32)
        ht = hidden[:, drows, :]
        out_part = place(dblocks, BLK, dcols, jnp.einsum('tsk,skn->tsn', ht, wd, precision=hi) * dlive[None, :, None])
        dyt = dy_blocks[:, dcols, :]
        dhid = place(hblocks, BLK, drows, jnp.einsum('tsn,skn->tsk', dyt, wd, precision=hi) * dlive[None, :, None])
        d_gate = (dhid * up * sig * (1.0 + gate * (1.0 - sig))).astype(jnp.bfloat16).astype(jnp.float32)
        d_up = (dhid * act).astype(jnp.bfloat16).astype(jnp.float32)
        dgt = d_gate[:, cols, :]
        dut = d_up[:, cols, :]
        back = jnp.einsum('tsn,skn->tsk', dgt, wg, precision=hi) + jnp.einsum('tsn,skn->tsk', dut, wu, precision=hi)
        in_part = place(dblocks, BLK, rows, back * live[None, :, None])
        gate_grad = group_grad(xt, dgt)
        up_grad = group_grad(xt, dut)
        down_grad = group_grad(ht, dyt)
        gate_step = (gate_grad * scale_root + decay_coef * wg) * live[:, None, None]
        up_step = (up_grad * scale_root + decay_coef * wu) * live[:, None, None]
        down_step = (down_grad * scale_root + decay_coef * wd) * dlive[:, None, None]
        return ((out_total + out_part, in_total + in_part), (gate_step, up_step, down_step))
    start = (jnp.zeros((ntok, dblocks, BLK), jnp.float32), jnp.zeros((ntok, dblocks, BLK), jnp.float32))
    sums, steps = lax.scan(one_device, start, jnp.arange(N_MP).astype(jnp.int32))
    ffn_out = sums[0].reshape(ntok, D).astype(jnp.bfloat16)
    input_grad = sums[1].reshape(ntok, D).astype(jnp.bfloat16)
    return (ffn_out, input_grad, steps[0], steps[1], steps[2])
```

```python
import functools
import math

import jax
import jax.numpy as jnp
from jax import lax
from jax.experimental import pallas as pl
from jax.experimental.pallas import tpu as pltpu
from jax.sharding import PartitionSpec as P

HID_DEV = 896
MESH = pl.DeviceIdType.MESH
F32 = jnp.float32
BF16 = jnp.bfloat16

decay_coef = 8.0


def ring_position(index, n):
    half, odd = index // 2, index % 2
    return (1 - odd) * half + odd * (n - 1 - half)


def ring_device(position, n):
    late = position // (n // 2)
    return (1 - late) * (2 * position) + late * (2 * (n - 1 - position) + 1)


def gather_kernel(n, x_ref, dy_ref, xf_ref, dyf_ref, send_sem, recv_sem, own_sem):
    me = lax.axis_index("mp")
    pos = ring_position(me, n)
    half = x_ref.shape[0] // 2
    target = [ring_device((pos + 1) % n, n), ring_device((pos + n - 1) % n, n)]

    barrier = pltpu.get_barrier_semaphore()
    for device in target:
        pl.semaphore_signal(barrier, inc=1, device_id={"mp": device}, device_id_type=MESH)
    pl.semaphore_wait(barrier, 2)

    pairs = ((x_ref, xf_ref), (dy_ref, dyf_ref))
    own = [
        pltpu.make_async_copy(shard, full.at[me], own_sem.at[a])
        for a, (shard, full) in enumerate(pairs)
    ]

    def hop(a, d, s):
        shard, full = pairs[a]
        rows = pl.ds(d * half, half)
        owner = ring_device((pos + (n - s if d == 0 else s)) % n, n)
        src = shard.at[rows] if s == 0 else full.at[owner, rows]
        return pltpu.make_async_remote_copy(
            src_ref=src,
            dst_ref=full.at[owner, rows],
            send_sem=send_sem.at[a, d, s],
            recv_sem=recv_sem.at[a, d, s],
            device_id={"mp": target[d]},
            device_id_type=MESH,
        )

    copies = {}
    for s in range(n - 1):
        for a in range(2):
            for d in range(2):
                if s > 0:
                    copies[a, d, s - 1].wait_recv()
                copies[a, d, s] = hop(a, d, s)
                copies[a, d, s].start()
        if s == 0:
            for copy in own:
                copy.start()
    for a in range(2):
        for d in range(2):
            copies[a, d, n - 2].wait_recv()
    for copy in own:
        copy.wait()
    for copy in copies.values():
        copy.wait_send()


def gather(tokens, out_grad, n):
    full = jax.ShapeDtypeStruct((n,) + tokens.shape, BF16)
    return pl.pallas_call(
        functools.partial(gather_kernel, n),
        out_shape=(full, full),
        in_specs=[pl.BlockSpec(memory_space=pl.ANY)] * 2,
        out_specs=(pl.BlockSpec(memory_space=pl.ANY),) * 2,
        scratch_shapes=[
            pltpu.SemaphoreType.DMA((2, 2, n - 1)),
            pltpu.SemaphoreType.DMA((2, 2, n - 1)),
            pltpu.SemaphoreType.DMA((2,)),
        ],
        compiler_params=pltpu.CompilerParams(collective_id=0, has_side_effects=True),
    )(tokens, out_grad)


GROUP = 4


def dot(left, right, contract):
    return lax.dot_general(left, right, (contract, ((), ())), preferred_element_type=F32)


def compute_kernel(
    rows_ref, cols_ref, count_ref, drows_ref, dcols_ref, dcount_ref,
    x_ref, dy_ref, wg_ref, wu_ref, wd_ref,
    out_ref, in_ref, grad_ref,
    gu_acc, dh_acc, hid, dgu, wide,
):
    blk = wg_ref.shape[-1]
    per = x_ref.shape[2] // blk
    count = count_ref[0]
    dcount = dcount_ref[0]
    steps = (count + GROUP - 1) // GROUP
    dsteps = (dcount + GROUP - 1) // GROUP

    def place(block):
        return block // per, pl.ds(pl.multiple_of((block % per) * blk, blk), blk)

    def tile(ref, block):
        part, lanes = place(block)
        return ref[part, :, lanes]

    def gated(s):
        both = jnp.concatenate([wg_ref[s], wu_ref[s]], axis=1)
        return jnp.where(s < count, both, jnp.zeros_like(both))

    def down(s):
        return jnp.where(s < dcount, wd_ref[s], jnp.zeros_like(wd_ref[s]))

    gu_acc[...] = jnp.zeros_like(gu_acc)
    dh_acc[...] = jnp.zeros_like(dh_acc)

    def forward(i, carry):
        slots = [i * GROUP + j for j in range(GROUP)]
        parts = [dot(tile(x_ref, rows_ref[s]), gated(s), ((1,), (0,))) for s in slots]
        for s, part in zip(slots, parts):
            gu_acc[cols_ref[s]] += part
        return carry

    lax.fori_loop(0, steps, forward, 0)

    def hidden_back(i, carry):
        slots = [i * GROUP + j for j in range(GROUP)]
        parts = [dot(tile(dy_ref, dcols_ref[s]), down(s), ((1,), (1,))) for s in slots]
        for s, part in zip(slots, parts):
            dh_acc[drows_ref[s]] += part
        return carry

    lax.fori_loop(0, dsteps, hidden_back, 0)

    def pointwise(h, carry):
        gate = gu_acc[h, :, :blk]
        up = gu_acc[h, :, blk:]
        dhid = dh_acc[h]
        sig = 1.0 / (1.0 + jnp.exp(-gate))
        act = gate * sig
        hid[h] = (act * up).astype(BF16)
        dgu[h, :, :blk] = (dhid * up * sig * (1.0 + gate * (1.0 - sig))).astype(BF16)
        dgu[h, :, blk:] = (dhid * act).astype(BF16)
        return carry

    lax.fori_loop(0, gu_acc.shape[0], pointwise, 0)

    def clear(p, carry):
        wide[p] = jnp.zeros(wide.shape[1:], F32)
        return carry

    lax.fori_loop(0, wide.shape[0], clear, 0)

    def down_step(i, carry):
        slots = [i * GROUP + j for j in range(GROUP)]
        hs = [hid[drows_ref[s]] for s in slots]
        parts = [dot(h, down(s), ((1,), (0,))) for s, h in zip(slots, hs)]
        for s, h in zip(slots, hs):
            grad_ref[2, s] = dot(h, tile(dy_ref, dcols_ref[s]), ((0,), (0,))).astype(BF16)
        for s, part in zip(slots, parts):
            at, lanes = place(dcols_ref[s])
            wide[at, :, lanes] += part
        return carry

    lax.fori_loop(0, dsteps, down_step, 0)

    def flush(ref):
        def body(p, carry):
            ref[p] = wide[p].astype(BF16)
            wide[p] = jnp.zeros(wide.shape[1:], F32)
            return carry
        lax.fori_loop(0, wide.shape[0], body, 0)

    flush(out_ref)

    def gate_step(i, carry):
        slots = [i * GROUP + j for j in range(GROUP)]
        gs = [dgu[cols_ref[s]] for s in slots]
        parts = [dot(g, gated(s), ((1,), (1,))) for s, g in zip(slots, gs)]
        for s, g in zip(slots, gs):
            both = dot(tile(x_ref, rows_ref[s]), g, ((0,), (0,))).astype(BF16)
            grad_ref[0, s] = both[:, :blk]
            grad_ref[1, s] = both[:, blk:]
        for s, part in zip(slots, parts):
            at, lanes = place(rows_ref[s])
            wide[at, :, lanes] += part
        return carry

    lax.fori_loop(0, steps, gate_step, 0)
    flush(in_ref)

    def dead(s, carry):
        @pl.when(s >= count)
        def _():
            grad_ref[0, s] = jnp.zeros((blk, blk), BF16)
            grad_ref[1, s] = jnp.zeros((blk, blk), BF16)

        @pl.when(s >= dcount)
        def _():
            grad_ref[2, s] = jnp.zeros((blk, blk), BF16)

        return carry

    lax.fori_loop(0, grad_ref.shape[1], dead, 0)


def compute(xf, dyf, wg, wu, wd, rows, cols, count, drows, dcols, dcount):
    n, ntok, width = xf.shape
    slots, blk, _ = wg.shape
    hblocks = HID_DEV // blk
    full = jax.ShapeDtypeStruct(xf.shape, BF16)
    return pl.pallas_call(
        compute_kernel,
        out_shape=(full, full, jax.ShapeDtypeStruct((3, slots, blk, blk), BF16)),
        in_specs=[pl.BlockSpec(memory_space=pltpu.SMEM)] * 6
        + [pl.BlockSpec(memory_space=pltpu.VMEM)] * 5,
        out_specs=(pl.BlockSpec(memory_space=pltpu.VMEM),) * 3,
        scratch_shapes=[
            pltpu.VMEM((hblocks, ntok, 2 * blk), F32),
            pltpu.VMEM((hblocks, ntok, blk), F32),
            pltpu.VMEM((hblocks, ntok, blk), BF16),
            pltpu.VMEM((hblocks, ntok, 2 * blk), BF16),
            pltpu.VMEM((n, ntok, width), F32),
        ],
        compiler_params=pltpu.CompilerParams(vmem_limit_bytes=56 << 20),
    )(rows, cols, count, drows, dcols, dcount, xf, dyf, wg, wu, wd)


def scatter_kernel(
    n, nd, op_ref, ip_ref, grad_ref, out_ref, in_ref, sum_ref,
    ring, pair, far, ring_send, ring_recv, pair_send, pair_recv, far_send, far_recv,
):
    me = lax.axis_index("mp")
    pos = ring_position(me, n)
    half = out_ref.shape[0] // 2
    target = [ring_device((pos + 1) % n, n), ring_device((pos + n - 1) % n, n)]
    dp = lax.axis_index("dp")
    ny = nd // 2
    y, core = dp // 2, dp % 2
    partner = 2 * y + (1 - core)
    ahead = 2 * ((y + 1) % ny) + core
    behind = 2 * ((y + ny - 1) % ny) + core

    barrier = pltpu.get_barrier_semaphore()
    greet = [{"mp": target[0]}, {"mp": target[1]}, {"dp": partner}, {"dp": ahead}]
    if ny > 2:
        greet.append({"dp": behind})
    for device in greet:
        pl.semaphore_signal(barrier, inc=1, device_id=device, device_id_type=MESH)
    pl.semaphore_wait(barrier, len(greet))

    parts = (op_ref, ip_ref)
    results = (out_ref, in_ref)
    started = []

    def remote(src, dst, send, recv, device):
        copy = pltpu.make_async_remote_copy(
            src_ref=src, dst_ref=dst, send_sem=send, recv_sem=recv,
            device_id=device, device_id_type=MESH,
        )
        copy.start()
        started.append(copy)
        return copy

    def chunk(d, s):
        return ring_device((pos + (2 * n - 1 - s if d == 0 else 1 + s)) % n, n)

    def ring_hop(a, d, s):
        rows = pl.ds(d * half, half)
        src = parts[a].at[chunk(d, 0), rows] if s == 0 else ring.at[a, d, s - 1]
        return remote(
            src, ring.at[a, d, s], ring_send.at[a, d, s], ring_recv.at[a, d, s], {"mp": target[d]}
        )

    def ring_add(a, d, s):
        own = chunk(d, s + 1)
        step = 32

        def body(i, carry):
            r = pl.multiple_of(i * step, step)
            mine = parts[a][own, pl.ds(d * half + r, step), :].astype(F32)
            total = (ring[a, d, s, pl.ds(r, step), :].astype(F32) + mine).astype(BF16)
            if s < n - 2:
                ring[a, d, s, pl.ds(r, step), :] = total
            else:
                results[a][pl.ds(d * half + r, step), :] = total
            return carry

        lax.fori_loop(0, half // step, body, 0)

    def group(t):
        return (y + 2 * ny - 1 - t) % ny

    hops = {}
    for d in range(2):
        for a in range(2):
            hops[a, d] = ring_hop(a, d, 0)
    pairs = {}
    for t in range(ny):
        for k in range(3):
            pairs[k, t] = remote(
                grad_ref.at[k, group(t), 1 - core], pair.at[k, group(t)],
                pair_send.at[k, t], pair_recv.at[k, t], {"dp": partner},
            )
    fars = {}

    def pair_add(k, t):
        pairs[k, t].wait_recv()
        g = group(t)
        if t > 0:
            fars[k, t - 1].wait_recv()

        def body(i, carry):
            total = pair[k, g, i].astype(F32) + grad_ref[k, g, core, i].astype(F32)
            if t > 0:
                total = total + far[k, t - 1, i].astype(F32)
            if t < ny - 1:
                pair[k, g, i] = total.astype(BF16)
            else:
                sum_ref[k, i] = total
            return carry

        lax.fori_loop(0, sum_ref.shape[1], body, 0)
        if t < ny - 1:
            fars[k, t] = remote(
                pair.at[k, g], far.at[k, t], far_send.at[k, t], far_recv.at[k, t], {"dp": ahead}
            )

    for k in range(3):
        pair_add(k, 0)
    for s in range(n - 1):
        for a in range(2):
            for d in range(2):
                hops[a, d].wait_recv()
                ring_add(a, d, s)
                if s < n - 2:
                    hops[a, d] = ring_hop(a, d, s + 1)
    for t in range(1, ny):
        for k in range(3):
            pair_add(k, t)
    for copy in started:
        copy.wait_send()


def scatter(out_part, in_part, grads, nd):
    n, ntok, width = out_part.shape
    _, slots, blk, _ = grads.shape
    share = slots // nd
    ny = nd // 2
    grads = grads.reshape(3, ny, 2, share, blk, blk)
    return pl.pallas_call(
        functools.partial(scatter_kernel, n, nd),
        out_shape=(
            jax.ShapeDtypeStruct((ntok, width), BF16),
            jax.ShapeDtypeStruct((ntok, width), BF16),
            jax.ShapeDtypeStruct((3, share, blk, blk), F32),
        ),
        in_specs=[pl.BlockSpec(memory_space=pltpu.VMEM)] * 3,
        out_specs=(pl.BlockSpec(memory_space=pltpu.VMEM),) * 3,
        scratch_shapes=[
            pltpu.VMEM((2, 2, n - 1, ntok // 2, width), BF16),
            pltpu.VMEM((3, ny, share, blk, blk), BF16),
            pltpu.VMEM((3, max(ny - 1, 1), share, blk, blk), BF16),
            pltpu.SemaphoreType.DMA((2, 2, n - 1)),
            pltpu.SemaphoreType.DMA((2, 2, n - 1)),
            pltpu.SemaphoreType.DMA((3, ny)),
            pltpu.SemaphoreType.DMA((3, ny)),
            pltpu.SemaphoreType.DMA((3, ny)),
            pltpu.SemaphoreType.DMA((3, ny)),
        ],
        compiler_params=pltpu.CompilerParams(
            collective_id=1, has_side_effects=True, vmem_limit_bytes=56 << 20
        ),
    )(out_part, in_part, grads)


def finish(summed, weights, count, scale_root):
    share = summed.shape[0]
    start = lax.axis_index("dp") * share
    own_w = lax.dynamic_slice_in_dim(weights, start, share, 0).astype(F32)
    live = start + jnp.arange(share) < count[0]
    return jnp.where(live[:, None, None], summed * scale_root + decay_coef * own_w, 0.0)[None]


def local(
    tokens, out_grad, w_gate, w_up, w_down, gu_rows, gu_cols, gu_count, dn_rows, dn_cols, dn_count
):
    n = lax.axis_size("mp")
    nd = lax.axis_size("dp")
    wg, wu, wd = w_gate[0], w_up[0], w_down[0]
    scale_root = 1.0 / math.sqrt(tokens.shape[0] * nd)
    xf, dyf = gather(tokens, out_grad, n)
    out_part, in_part, grads = compute(
        xf, dyf, wg, wu, wd, gu_rows[0], gu_cols[0], gu_count, dn_rows[0], dn_cols[0], dn_count
    )
    ffn_out, input_grad, summed = scatter(out_part, in_part, grads, nd)
    gate_step = finish(summed[0], wg, gu_count, scale_root)
    up_step = finish(summed[1], wu, gu_count, scale_root)
    down_step = finish(summed[2], wd, dn_count, scale_root)
    return (ffn_out, input_grad, gate_step, up_step, down_step)


def solution(mesh):
    in_specs = (
        P("dp", "mp"),
        P("dp", "mp"),
        P("mp", None, None, None),
        P("mp", None, None, None),
        P("mp", None, None, None),
        P("mp", None),
        P("mp", None),
        P("mp"),
        P("mp", None),
        P("mp", None),
        P("mp"),
    )
    out_specs = (
        P("dp", "mp"),
        P("dp", "mp"),
        P("mp", "dp", None, None),
        P("mp", "dp", None, None),
        P("mp", "dp", None, None),
    )
    return jax.shard_map(local, mesh=mesh, in_specs=in_specs, out_specs=out_specs, check_vma=False)
```

```python
import functools
import math

import jax
import jax.numpy as jnp
from jax import lax
from jax.experimental import pallas as pl
from jax.experimental.pallas import tpu as pltpu
from jax.sharding import PartitionSpec as P

HID_DEV = 896
MESH = pl.DeviceIdType.MESH
F32 = jnp.float32
BF16 = jnp.bfloat16

decay_coef = 8.0


def ring_position(index, n):
    half, odd = index // 2, index % 2
    return (1 - odd) * half + odd * (n - 1 - half)


def ring_device(position, n):
    late = position // (n // 2)
    return (1 - late) * (2 * position) + late * (2 * (n - 1 - position) + 1)


def dot(left, right, contract):
    return lax.dot_general(left, right, (contract, ((), ())), preferred_element_type=F32)


def layer_kernel(
    n, nd, gtab_ref, dtab_ref, rows_ref, cols_ref, drows_ref, dcols_ref,
    x_ref, dy_ref, wg_ref, wu_ref, wd_ref,
    out_ref, in_ref, sum_ref,
    xs, dys, wgs, wus, wds, gu_acc, dh_acc, hid, dgu, hid_tiles, dgu_tiles, first, own, ring, grad, pair, far,
    own_sem, w_sem, ag_send, ag_recv, ring_send, ring_recv, pair_send, pair_recv, far_send, far_recv,
):
    blk = wg_ref.shape[-1]
    ntok, width = x_ref.shape
    per = width // blk
    hblocks = gu_acc.shape[0]
    half = ntok // 2
    me = lax.axis_index("mp")
    pos = ring_position(me, n)
    target = [ring_device((pos + 1) % n, n), ring_device((pos + n - 1) % n, n)]
    dp = lax.axis_index("dp")
    ny = nd // 2
    y, core = dp // 2, dp % 2
    partner = 2 * y + (1 - core)
    ahead = 2 * ((y + 1) % ny) + core
    behind = 2 * ((y + ny - 1) % ny) + core
    started = []

    loads = [
        pltpu.make_async_copy(w, held.at[pl.ds(1, w.shape[0])], w_sem.at[k])
        for k, (w, held) in enumerate(((wg_ref, wgs), (wu_ref, wus), (wd_ref, wds)))
    ]
    full = (xs, dys)
    owns = [
        pltpu.make_async_copy(
            shard.at[:, pl.ds(f * blk, blk)], full[a].at[me * per + f], own_sem.at[a, f]
        )
        for f in range(per)
        for a, shard in enumerate((x_ref, dy_ref))
    ]
    for copy in owns + loads:
        copy.start()

    barrier = pltpu.get_barrier_semaphore()
    greet = [{"mp": target[0]}, {"mp": target[1]}, {"dp": partner}, {"dp": ahead}]
    if ny > 2:
        greet.append({"dp": behind})
    for device in greet:
        pl.semaphore_signal(barrier, inc=1, device_id=device, device_id_type=MESH)
    pl.semaphore_wait(barrier, len(greet))

    def remote(src, dst, send, recv, device):
        copy = pltpu.make_async_remote_copy(
            src_ref=src, dst_ref=dst, send_sem=send, recv_sem=recv,
            device_id=device, device_id_type=MESH,
        )
        copy.start()
        started.append(copy)
        return copy

    def owner(a, s):
        return ring_device((pos + (n - s if a == 0 else s)) % n, n)

    def gather_hop(a, s, h):
        blocks = pl.ds(owner(a, s) * per + h * (per // 2), per // 2)
        return remote(
            full[a].at[blocks], full[a].at[blocks],
            ag_send.at[a, s, h], ag_recv.at[a, s, h], {"mp": target[a]},
        )

    def features(a, o):
        return jnp.concatenate([full[a][o * per + f] for f in range(per)], axis=1)

    def gate_up(o):
        def body(h, carry):
            tabs = [gtab_ref[(o * per + f) * hblocks + h] for f in range(per)]
            rhs = jnp.concatenate(
                [jnp.concatenate([wgs[t], wus[t]], axis=1) for t in tabs], axis=0
            )
            gu_acc[h] += dot(features(0, o), rhs, ((1,), (0,)))
            return carry

        lax.fori_loop(0, hblocks, body, 0)

    def hidden_back(o):
        def body(h, carry):
            tabs = [dtab_ref[(o * per + f) * hblocks + h] for f in range(per)]
            rhs = jnp.concatenate([wds[t] for t in tabs], axis=1)
            dh_acc[h] += dot(features(1, o), rhs, ((1,), (1,)))
            return carry

        lax.fori_loop(0, hblocks, body, 0)

    for copy in owns:
        copy.wait()
    hops = {}
    for h in range(2):
        for a in range(2):
            hops[a, h] = gather_hop(a, 0, h)
    gu_acc[...] = jnp.zeros_like(gu_acc)
    dh_acc[...] = jnp.zeros_like(dh_acc)
    for held in (wgs, wus, wds):
        held[0] = jnp.zeros((blk, blk), BF16)
    for copy in loads:
        copy.wait()
    gate_up(me)
    hidden_back(me)
    for s in range(1, n):
        for h in range(2):
            for a in range(2):
                hops[a, h].wait_recv()
                if s < n - 1:
                    hops[a, h] = gather_hop(a, s, h)
        gate_up(owner(0, s))
        hidden_back(owner(1, s))

    for h in range(hblocks):
        gate = gu_acc[h, :, :blk]
        up = gu_acc[h, :, blk:]
        dhid = dh_acc[h]
        sig = 1.0 / (1.0 + jnp.exp(-gate))
        act = gate * sig
        hidden = (act * up).astype(BF16)
        d_gate = (dhid * up * sig * (1.0 + gate * (1.0 - sig))).astype(BF16)
        d_up = (dhid * act).astype(BF16)
        hid[:, h * blk:(h + 1) * blk] = hidden
        hid_tiles[h] = hidden
        both = jnp.concatenate([d_gate, d_up], axis=1)
        dgu[:, 2 * h * blk:2 * (h + 1) * blk] = both
        dgu_tiles[h] = both

    def chunk(a, s):
        return ring_device((pos + (2 * n - 1 - s if a == 0 else 1 + s)) % n, n)

    def out_chunk(ref, o):
        def body(f, carry):
            base = (o * per + f) * hblocks
            rhs = jnp.concatenate([wds[dtab_ref[base + h]] for h in range(hblocks)], axis=0)
            lanes = pl.ds(pl.multiple_of(f * blk, blk), blk)
            ref[:, lanes] = dot(hid[...], rhs, ((1,), (0,))).astype(ref.dtype)
            return carry

        lax.fori_loop(0, per, body, 0)

    def in_chunk(ref, o):
        def body(f, carry):
            base = (o * per + f) * hblocks
            tabs = [gtab_ref[base + h] for h in range(hblocks)]
            rhs = jnp.concatenate([held[t] for t in tabs for held in (wgs, wus)], axis=1)
            lanes = pl.ds(pl.multiple_of(f * blk, blk), blk)
            ref[:, lanes] = dot(dgu[...], rhs, ((1,), (1,))).astype(ref.dtype)
            return carry

        lax.fori_loop(0, per, body, 0)

    own_chunk = (out_chunk, in_chunk)
    results = (out_ref, in_ref)

    def ring_hop(a, s, h):
        rows = pl.ds(h * half, half)
        src = first.at[a, rows] if s == 0 else ring.at[a, s - 1, rows]
        return remote(
            src, ring.at[a, s, rows], ring_send.at[a, s, h], ring_recv.at[a, s, h], {"mp": target[a]}
        )

    def ring_add(a, s, h):
        step = 32

        def body(i, carry):
            r = pl.multiple_of(h * half + i * step, step)
            total = (ring[a, s, pl.ds(r, step), :].astype(F32) + own[a, pl.ds(r, step), :]).astype(BF16)
            if s < n - 2:
                ring[a, s, pl.ds(r, step), :] = total
            else:
                results[a][pl.ds(r, step), :] = total
            return carry

        lax.fori_loop(0, half // step, body, 0)

    def ring_step(s):
        for h in range(2):
            for a in range(2):
                hops[a, h].wait_recv()
                ring_add(a, s, h)
                if s < n - 2:
                    hops[a, h] = ring_hop(a, s + 1, h)
        if s < n - 2:
            for a in range(2):
                own_chunk[a](own.at[a], chunk(a, s + 2))

    share = grad.shape[3]

    def group(t):
        return (y + 2 * ny - 1 - t) % ny

    def slot_grads(t, c):
        g = group(t)
        base = (2 * g + c) * share
        unit = 4

        def body(i, carry):
            for j in range(unit):
                e = i * unit + j
                s = base + e
                down = dot(hid_tiles[drows_ref[s]], dys[dcols_ref[s]], ((0,), (0,)))
                both = dot(xs[rows_ref[s]], dgu_tiles[cols_ref[s]], ((0,), (0,)))
                grad[0, g, c, e] = both[:, :blk].astype(BF16)
                grad[1, g, c, e] = both[:, blk:].astype(BF16)
                grad[2, g, c, e] = down.astype(BF16)
            return carry

        lax.fori_loop(0, share // unit, body, 0)

    pairs = {}
    fars = {}

    def give(t):
        slot_grads(t, 1 - core)
        g = group(t)
        for k in range(3):
            pairs[k, t] = remote(
                grad.at[k, g, 1 - core], pair.at[k, g],
                pair_send.at[k, t], pair_recv.at[k, t], {"dp": partner},
            )

    def keep(t):
        slot_grads(t, core)

    def pair_add(t):
        g = group(t)
        for k in range(3):
            pairs[k, t].wait_recv()
            if t > 0:
                fars[k, t - 1].wait_recv()

            def body(i, carry):
                total = pair[k, g, i].astype(F32) + grad[k, g, core, i].astype(F32)
                if t > 0:
                    total = total + far[k, t - 1, i].astype(F32)
                if t < ny - 1:
                    pair[k, g, i] = total.astype(BF16)
                else:
                    sum_ref[k, i] = total
                return carry

            lax.fori_loop(0, share, body, 0)
            if t < ny - 1:
                fars[k, t] = remote(
                    pair.at[k, g], far.at[k, t], far_send.at[k, t], far_recv.at[k, t], {"dp": ahead}
                )

    for a in range(2):
        own_chunk[a](first.at[a], chunk(a, 0))
        for h in range(2):
            hops[a, h] = ring_hop(a, 0, h)
    give(0)
    keep(0)
    for a in range(2):
        own_chunk[a](own.at[a], chunk(a, 1))
    tasks = [functools.partial(pair_add, 0)]
    for t in range(1, ny):
        tasks += [functools.partial(give, t), functools.partial(keep, t)]
        if t < ny - 1:
            tasks.append(functools.partial(pair_add, t))
    for s in range(n - 1):
        ring_step(s)
        if tasks:
            tasks.pop(0)()
    for task in tasks:
        task()
    pair_add(ny - 1)
    for copy in started:
        copy.wait_send()


def layer(tokens, out_grad, wg, wu, wd, gtab, dtab, rows, cols, drows, dcols, n, nd):
    ntok, width = tokens.shape
    slots, blk, _ = wg.shape
    share = slots // nd
    ny = nd // 2
    hblocks = HID_DEV // blk
    return pl.pallas_call(
        functools.partial(layer_kernel, n, nd),
        out_shape=(
            jax.ShapeDtypeStruct((ntok, width), BF16),
            jax.ShapeDtypeStruct((ntok, width), BF16),
            jax.ShapeDtypeStruct((3, share, blk, blk), F32),
        ),
        in_specs=[pl.BlockSpec(memory_space=pltpu.SMEM)] * 6
        + [pl.BlockSpec(memory_space=pl.ANY)] * 5,
        out_specs=(pl.BlockSpec(memory_space=pltpu.VMEM),) * 3,
        scratch_shapes=[
            pltpu.VMEM((n * width // blk, ntok, blk), BF16),
            pltpu.VMEM((n * width // blk, ntok, blk), BF16),
            pltpu.VMEM((slots + 1, blk, blk), BF16),
            pltpu.VMEM((slots + 1, blk, blk), BF16),
            pltpu.VMEM((slots + 1, blk, blk), BF16),
            pltpu.VMEM((hblocks, ntok, 2 * blk), F32),
            pltpu.VMEM((hblocks, ntok, blk), F32),
            pltpu.VMEM((ntok, hblocks * blk), BF16),
            pltpu.VMEM((ntok, 2 * hblocks * blk), BF16),
            pltpu.VMEM((hblocks, ntok, blk), BF16),
            pltpu.VMEM((hblocks, ntok, 2 * blk), BF16),
            pltpu.VMEM((2, ntok, width), BF16),
            pltpu.VMEM((2, ntok, width), F32),
            pltpu.VMEM((2, n - 1, ntok, width), BF16),
            pltpu.VMEM((3, ny, 2, share, blk, blk), BF16),
            pltpu.VMEM((3, ny, share, blk, blk), BF16),
            pltpu.VMEM((3, max(ny - 1, 1), share, blk, blk), BF16),
            pltpu.SemaphoreType.DMA((2, width // blk)),
            pltpu.SemaphoreType.DMA((3,)),
            pltpu.SemaphoreType.DMA((2, n - 1, 2)),
            pltpu.SemaphoreType.DMA((2, n - 1, 2)),
            pltpu.SemaphoreType.DMA((2, n - 1, 2)),
            pltpu.SemaphoreType.DMA((2, n - 1, 2)),
            pltpu.SemaphoreType.DMA((3, ny)),
            pltpu.SemaphoreType.DMA((3, ny)),
            pltpu.SemaphoreType.DMA((3, ny)),
            pltpu.SemaphoreType.DMA((3, ny)),
        ],
        compiler_params=pltpu.CompilerParams(
            collective_id=0, has_side_effects=True, vmem_limit_bytes=58 << 20
        ),
    )(gtab, dtab, rows, cols, drows, dcols, tokens, out_grad, wg, wu, wd)


def slot_table(features, hidden, count, dblocks, hblocks):
    slot = jnp.arange(features.shape[0])
    key = jnp.where(slot < count[0], features * hblocks + hidden, -1)
    hit = key[None, :] == jnp.arange(dblocks * hblocks)[:, None]
    return jnp.sum(jnp.where(hit, slot[None, :] + 1, 0), axis=1).astype(jnp.int32)


def finish(summed, weights, count, scale_root):
    share = summed.shape[0]
    start = lax.axis_index("dp") * share
    own_w = lax.dynamic_slice_in_dim(weights, start, share, 0).astype(F32)
    live = start + jnp.arange(share) < count[0]
    return jnp.where(live[:, None, None], summed * scale_root + decay_coef * own_w, 0.0)[None]


def local(
    tokens, out_grad, w_gate, w_up, w_down, gu_rows, gu_cols, gu_count, dn_rows, dn_cols, dn_count
):
    n = lax.axis_size("mp")
    nd = lax.axis_size("dp")
    wg, wu, wd = w_gate[0], w_up[0], w_down[0]
    scale_root = 1.0 / math.sqrt(tokens.shape[0] * nd)
    blk = wg.shape[-1]
    dblocks = tokens.shape[1] * n // blk
    hblocks = HID_DEV // blk
    gtab = slot_table(gu_rows[0], gu_cols[0], gu_count, dblocks, hblocks)
    dtab = slot_table(dn_cols[0], dn_rows[0], dn_count, dblocks, hblocks)
    ffn_out, input_grad, summed = layer(
        tokens, out_grad, wg, wu, wd, gtab, dtab,
        gu_rows[0], gu_cols[0], dn_rows[0], dn_cols[0], n, nd,
    )
    gate_step = finish(summed[0], wg, gu_count, scale_root)
    up_step = finish(summed[1], wu, gu_count, scale_root)
    down_step = finish(summed[2], wd, dn_count, scale_root)
    return (ffn_out, input_grad, gate_step, up_step, down_step)


def solution(mesh):
    in_specs = (
        P("dp", "mp"),
        P("dp", "mp"),
        P("mp", None, None, None),
        P("mp", None, None, None),
        P("mp", None, None, None),
        P("mp", None),
        P("mp", None),
        P("mp"),
        P("mp", None),
        P("mp", None),
        P("mp"),
    )
    out_specs = (
        P("dp", "mp"),
        P("dp", "mp"),
        P("mp", "dp", None, None),
        P("mp", "dp", None, None),
        P("mp", "dp", None, None),
    )
    return jax.shard_map(local, mesh=mesh, in_specs=in_specs, out_specs=out_specs, check_vma=False)
```

```python
import functools
import math

import jax
import jax.numpy as jnp
from jax import lax
from jax.experimental import pallas as pl
from jax.experimental.pallas import tpu as pltpu
from jax.sharding import PartitionSpec as P

HID_DEV = 896
MESH = pl.DeviceIdType.MESH
F32 = jnp.float32
BF16 = jnp.bfloat16

decay_coef = 8.0


def ring_position(index, n):
    half, odd = index // 2, index % 2
    return (1 - odd) * half + odd * (n - 1 - half)


def ring_device(position, n):
    late = position // (n // 2)
    return (1 - late) * (2 * position) + late * (2 * (n - 1 - position) + 1)


def dot(left, right, contract):
    return lax.dot_general(left, right, (contract, ((), ())), preferred_element_type=F32)


def layer_kernel(
    n, nd, gtab_ref, dtab_ref, rows_ref, cols_ref, drows_ref, dcols_ref,
    x_ref, dy_ref, wg_ref, wu_ref, wd_ref,
    out_ref, in_ref, sum_ref,
    xs, dys, wgs, wus, wds, gu_acc, dh_acc, hid, dgu, hid_tiles, dgu_tiles, first, own, ring, grad, pair, far,
    own_sem, w_sem, ag_send, ag_recv, ring_send, ring_recv, pair_send, pair_recv, far_send, far_recv,
):
    blk = wg_ref.shape[-1]
    ntok, width = x_ref.shape
    per = width // blk
    hblocks = gu_acc.shape[0]
    half = ntok // 2
    me = lax.axis_index("mp")
    pos = ring_position(me, n)
    target = [ring_device((pos + 1) % n, n), ring_device((pos + n - 1) % n, n)]
    dp = lax.axis_index("dp")
    ny = nd // 2
    y, core = dp // 2, dp % 2
    partner = 2 * y + (1 - core)
    ahead = 2 * ((y + 1) % ny) + core
    behind = 2 * ((y + ny - 1) % ny) + core
    started = []

    loads = [
        pltpu.make_async_copy(w, held.at[pl.ds(1, w.shape[0])], w_sem.at[k])
        for k, (w, held) in enumerate(((wg_ref, wgs), (wu_ref, wus), (wd_ref, wds)))
    ]
    full = (xs, dys)
    owns = [
        pltpu.make_async_copy(
            shard.at[:, pl.ds(f * blk, blk)], full[a].at[me * per + f], own_sem.at[a, f]
        )
        for f in range(per)
        for a, shard in enumerate((x_ref, dy_ref))
    ]
    for copy in owns + loads:
        copy.start()

    barrier = pltpu.get_barrier_semaphore()
    greet = [{"mp": target[0]}, {"mp": target[1]}, {"dp": partner}, {"dp": ahead}]
    if ny > 2:
        greet.append({"dp": behind})
    for device in greet:
        pl.semaphore_signal(barrier, inc=1, device_id=device, device_id_type=MESH)
    pl.semaphore_wait(barrier, len(greet))

    def remote(src, dst, send, recv, device):
        copy = pltpu.make_async_remote_copy(
            src_ref=src, dst_ref=dst, send_sem=send, recv_sem=recv,
            device_id=device, device_id_type=MESH,
        )
        copy.start()
        started.append(copy)
        return copy

    def owner(a, s):
        return ring_device((pos + (n - s if a == 0 else s)) % n, n)

    def gather_hop(a, s, h):
        blocks = pl.ds(owner(a, s) * per + h * (per // 2), per // 2)
        return remote(
            full[a].at[blocks], full[a].at[blocks],
            ag_send.at[a, s, h], ag_recv.at[a, s, h], {"mp": target[a]},
        )

    def features(a, o):
        return jnp.concatenate([full[a][o * per + f] for f in range(per)], axis=1)

    def gate_up(o):
        def body(h, carry):
            tabs = [gtab_ref[(o * per + f) * hblocks + h] for f in range(per)]
            rhs = jnp.concatenate(
                [jnp.concatenate([wgs[t], wus[t]], axis=1) for t in tabs], axis=0
            )
            gu_acc[h] += dot(features(0, o), rhs, ((1,), (0,)))
            return carry

        lax.fori_loop(0, hblocks, body, 0)

    def hidden_back(o):
        def body(h, carry):
            tabs = [dtab_ref[(o * per + f) * hblocks + h] for f in range(per)]
            rhs = jnp.concatenate([wds[t] for t in tabs], axis=1)
            dh_acc[h] += dot(features(1, o), rhs, ((1,), (1,)))
            return carry

        lax.fori_loop(0, hblocks, body, 0)

    for copy in owns:
        copy.wait()
    hops = {}
    for h in range(2):
        for a in range(2):
            hops[a, h] = gather_hop(a, 0, h)
    gu_acc[...] = jnp.zeros_like(gu_acc)
    dh_acc[...] = jnp.zeros_like(dh_acc)
    for held in (wgs, wus, wds):
        held[0] = jnp.zeros((blk, blk), BF16)
    for copy in loads:
        copy.wait()
    gate_up(me)
    hidden_back(me)
    for s in range(1, n):
        for h in range(2):
            for a in range(2):
                hops[a, h].wait_recv()
                if s < n - 1:
                    hops[a, h] = gather_hop(a, s, h)
        gate_up(owner(0, s))
        hidden_back(owner(1, s))

    for h in range(hblocks):
        gate = gu_acc[h, :, :blk]
        up = gu_acc[h, :, blk:]
        dhid = dh_acc[h]
        sig = 1.0 / (1.0 + jnp.exp(-gate))
        act = gate * sig
        hidden = (act * up).astype(BF16)
        d_gate = (dhid * up * sig * (1.0 + gate * (1.0 - sig))).astype(BF16)
        d_up = (dhid * act).astype(BF16)
        hid[:, h * blk:(h + 1) * blk] = hidden
        hid_tiles[h] = hidden
        both = jnp.concatenate([d_gate, d_up], axis=1)
        dgu[:, 2 * h * blk:2 * (h + 1) * blk] = both
        dgu_tiles[h] = both

    def chunk(a, s):
        return ring_device((pos + (2 * n - 1 - s if a == 0 else 1 + s)) % n, n)

    def out_chunk(ref, o):
        def body(f, carry):
            base = (o * per + 2 * f) * hblocks
            rhs = jnp.concatenate(
                [
                    jnp.concatenate([wds[dtab_ref[base + j * hblocks + h]] for j in range(2)], axis=1)
                    for h in range(hblocks)
                ],
                axis=0,
            )
            lanes = pl.ds(pl.multiple_of(f * 2 * blk, 2 * blk), 2 * blk)
            ref[:, lanes] = dot(hid[...], rhs, ((1,), (0,))).astype(ref.dtype)
            return carry

        lax.fori_loop(0, per // 2, body, 0)

    def in_chunk(ref, o):
        def body(f, carry):
            base = (o * per + 2 * f) * hblocks
            rhs = jnp.concatenate(
                [
                    jnp.concatenate(
                        [
                            held[t]
                            for t in [gtab_ref[base + j * hblocks + h] for h in range(hblocks)]
                            for held in (wgs, wus)
                        ],
                        axis=1,
                    )
                    for j in range(2)
                ],
                axis=0,
            )
            lanes = pl.ds(pl.multiple_of(f * 2 * blk, 2 * blk), 2 * blk)
            ref[:, lanes] = dot(dgu[...], rhs, ((1,), (1,))).astype(ref.dtype)
            return carry

        lax.fori_loop(0, per // 2, body, 0)

    own_chunk = (out_chunk, in_chunk)
    results = (out_ref, in_ref)

    def ring_hop(a, s, h):
        rows = pl.ds(h * half, half)
        src = first.at[a, rows] if s == 0 else ring.at[a, s - 1, rows]
        return remote(
            src, ring.at[a, s, rows], ring_send.at[a, s, h], ring_recv.at[a, s, h], {"mp": target[a]}
        )

    def ring_add(a, s, h):
        step = 32

        def body(i, carry):
            r = pl.multiple_of(h * half + i * step, step)
            total = (ring[a, s, pl.ds(r, step), :].astype(F32) + own[a, pl.ds(r, step), :]).astype(BF16)
            if s < n - 2:
                ring[a, s, pl.ds(r, step), :] = total
            else:
                results[a][pl.ds(r, step), :] = total
            return carry

        lax.fori_loop(0, half // step, body, 0)

    def ring_step(s):
        for h in range(2):
            for a in range(2):
                hops[a, h].wait_recv()
                ring_add(a, s, h)
                if s < n - 2:
                    hops[a, h] = ring_hop(a, s + 1, h)
        if s < n - 2:
            for a in range(2):
                own_chunk[a](own.at[a], chunk(a, s + 2))

    share = grad.shape[3]

    def group(t):
        return (y + 2 * ny - 1 - t) % ny

    def slot_grads(t, c):
        g = group(t)
        base = (2 * g + c) * share
        unit = 4

        def body(i, carry):
            for j in range(unit):
                e = i * unit + j
                s = base + e
                down = dot(hid_tiles[drows_ref[s]], dys[dcols_ref[s]], ((0,), (0,)))
                both = dot(xs[rows_ref[s]], dgu_tiles[cols_ref[s]], ((0,), (0,)))
                grad[0, g, c, e] = both[:, :blk].astype(BF16)
                grad[1, g, c, e] = both[:, blk:].astype(BF16)
                grad[2, g, c, e] = down.astype(BF16)
            return carry

        lax.fori_loop(0, share // unit, body, 0)

    pairs = {}
    fars = {}

    def give(t):
        slot_grads(t, 1 - core)
        g = group(t)
        for k in range(3):
            pairs[k, t] = remote(
                grad.at[k, g, 1 - core], pair.at[k, g],
                pair_send.at[k, t], pair_recv.at[k, t], {"dp": partner},
            )

    def keep(t):
        slot_grads(t, core)

    def pair_add(t):
        g = group(t)
        for k in range(3):
            pairs[k, t].wait_recv()
            if t > 0:
                fars[k, t - 1].wait_recv()

            def body(i, carry):
                total = pair[k, g, i].astype(F32) + grad[k, g, core, i].astype(F32)
                if t > 0:
                    total = total + far[k, t - 1, i].astype(F32)
                if t < ny - 1:
                    pair[k, g, i] = total.astype(BF16)
                else:
                    sum_ref[k, i] = total
                return carry

            lax.fori_loop(0, share, body, 0)
            if t < ny - 1:
                fars[k, t] = remote(
                    pair.at[k, g], far.at[k, t], far_send.at[k, t], far_recv.at[k, t], {"dp": ahead}
                )

    for a in range(2):
        own_chunk[a](first.at[a], chunk(a, 0))
        for h in range(2):
            hops[a, h] = ring_hop(a, 0, h)
    give(0)
    keep(0)
    for a in range(2):
        own_chunk[a](own.at[a], chunk(a, 1))
    pair_add(0)
    tasks = []
    for t in range(1, ny):
        tasks += [functools.partial(give, t), functools.partial(keep, t)]
        if t < ny - 1:
            tasks.append(functools.partial(pair_add, t))
    for s in range(n - 1):
        ring_step(s)
        if tasks:
            tasks.pop(0)()
    for task in tasks:
        task()
    pair_add(ny - 1)
    for copy in started:
        copy.wait_send()


def layer(tokens, out_grad, wg, wu, wd, gtab, dtab, rows, cols, drows, dcols, n, nd):
    ntok, width = tokens.shape
    slots, blk, _ = wg.shape
    share = slots // nd
    ny = nd // 2
    hblocks = HID_DEV // blk
    return pl.pallas_call(
        functools.partial(layer_kernel, n, nd),
        out_shape=(
            jax.ShapeDtypeStruct((ntok, width), BF16),
            jax.ShapeDtypeStruct((ntok, width), BF16),
            jax.ShapeDtypeStruct((3, share, blk, blk), F32),
        ),
        in_specs=[pl.BlockSpec(memory_space=pltpu.SMEM)] * 6
        + [pl.BlockSpec(memory_space=pl.ANY)] * 5,
        out_specs=(pl.BlockSpec(memory_space=pltpu.VMEM),) * 3,
        scratch_shapes=[
            pltpu.VMEM((n * width // blk, ntok, blk), BF16),
            pltpu.VMEM((n * width // blk, ntok, blk), BF16),
            pltpu.VMEM((slots + 1, blk, blk), BF16),
            pltpu.VMEM((slots + 1, blk, blk), BF16),
            pltpu.VMEM((slots + 1, blk, blk), BF16),
            pltpu.VMEM((hblocks, ntok, 2 * blk), F32),
            pltpu.VMEM((hblocks, ntok, blk), F32),
            pltpu.VMEM((ntok, hblocks * blk), BF16),
            pltpu.VMEM((ntok, 2 * hblocks * blk), BF16),
            pltpu.VMEM((hblocks, ntok, blk), BF16),
            pltpu.VMEM((hblocks, ntok, 2 * blk), BF16),
            pltpu.VMEM((2, ntok, width), BF16),
            pltpu.VMEM((2, ntok, width), F32),
            pltpu.VMEM((2, n - 1, ntok, width), BF16),
            pltpu.VMEM((3, ny, 2, share, blk, blk), BF16),
            pltpu.VMEM((3, ny, share, blk, blk), BF16),
            pltpu.VMEM((3, max(ny - 1, 1), share, blk, blk), BF16),
            pltpu.SemaphoreType.DMA((2, width // blk)),
            pltpu.SemaphoreType.DMA((3,)),
            pltpu.SemaphoreType.DMA((2, n - 1, 2)),
            pltpu.SemaphoreType.DMA((2, n - 1, 2)),
            pltpu.SemaphoreType.DMA((2, n - 1, 2)),
            pltpu.SemaphoreType.DMA((2, n - 1, 2)),
            pltpu.SemaphoreType.DMA((3, ny)),
            pltpu.SemaphoreType.DMA((3, ny)),
            pltpu.SemaphoreType.DMA((3, ny)),
            pltpu.SemaphoreType.DMA((3, ny)),
        ],
        compiler_params=pltpu.CompilerParams(
            collective_id=0, has_side_effects=True, vmem_limit_bytes=58 << 20
        ),
    )(gtab, dtab, rows, cols, drows, dcols, tokens, out_grad, wg, wu, wd)


def slot_table(features, hidden, count, dblocks, hblocks):
    slot = jnp.arange(features.shape[0])
    key = jnp.where(slot < count[0], features * hblocks + hidden, -1)
    hit = key[None, :] == jnp.arange(dblocks * hblocks)[:, None]
    return jnp.sum(jnp.where(hit, slot[None, :] + 1, 0), axis=1).astype(jnp.int32)


def finish(summed, weights, count, scale_root):
    share = summed.shape[0]
    start = lax.axis_index("dp") * share
    own_w = lax.dynamic_slice_in_dim(weights, start, share, 0).astype(F32)
    live = start + jnp.arange(share) < count[0]
    return jnp.where(live[:, None, None], summed * scale_root + decay_coef * own_w, 0.0)[None]


def local(
    tokens, out_grad, w_gate, w_up, w_down, gu_rows, gu_cols, gu_count, dn_rows, dn_cols, dn_count
):
    n = lax.axis_size("mp")
    nd = lax.axis_size("dp")
    wg, wu, wd = w_gate[0], w_up[0], w_down[0]
    scale_root = 1.0 / math.sqrt(tokens.shape[0] * nd)
    blk = wg.shape[-1]
    dblocks = tokens.shape[1] * n // blk
    hblocks = HID_DEV // blk
    gtab = slot_table(gu_rows[0], gu_cols[0], gu_count, dblocks, hblocks)
    dtab = slot_table(dn_cols[0], dn_rows[0], dn_count, dblocks, hblocks)
    ffn_out, input_grad, summed = layer(
        tokens, out_grad, wg, wu, wd, gtab, dtab,
        gu_rows[0], gu_cols[0], dn_rows[0], dn_cols[0], n, nd,
    )
    gate_step = finish(summed[0], wg, gu_count, scale_root)
    up_step = finish(summed[1], wu, gu_count, scale_root)
    down_step = finish(summed[2], wd, dn_count, scale_root)
    return (ffn_out, input_grad, gate_step, up_step, down_step)


def solution(mesh):
    in_specs = (
        P("dp", "mp"),
        P("dp", "mp"),
        P("mp", None, None, None),
        P("mp", None, None, None),
        P("mp", None, None, None),
        P("mp", None),
        P("mp", None),
        P("mp"),
        P("mp", None),
        P("mp", None),
        P("mp"),
    )
    out_specs = (
        P("dp", "mp"),
        P("dp", "mp"),
        P("mp", "dp", None, None),
        P("mp", "dp", None, None),
        P("mp", "dp", None, None),
    )
    return jax.shard_map(local, mesh=mesh, in_specs=in_specs, out_specs=out_specs, check_vma=False)
```
